512 devices in a mesh: blk: 32 (over x, y_lo, core), fsdp: 16 (over z, y_hi).
Axes of the slice: x: 4, y: 8 (y_hi: 2, y_lo: 4; y = y_hi * 4 + y_lo), z: 8, core: 2. Of those that a mesh axis runs over, the one named last changes fastest.
Arguments:
- decoder_states: bfloat16 [8192, 4096], P('blk', 'fsdp'), may hold values from -10 to 10
- w_query: bfloat16 [4096, 4096], P('blk', 'fsdp'), may hold values from -0.09375 to 0.09375
- w_out_t: bfloat16 [4096, 4096], P('blk', 'fsdp'), may hold values from -0.1875 to 0.1875
- enc_keys: bfloat16 [8192, 4096], P('blk', 'fsdp'), may hold values from -80 to 80
- enc_values: bfloat16 [8192, 4096], P('blk', 'fsdp'), may hold values from -6 to 6
Outputs:
- attended: bfloat16 [8192, 4096], P(('blk', 'fsdp'))
The draws below stay inside these ranges and needn't reach their ends.
All inputs are finite; a program needn't handle non-finite values.
Results may differ from the reference program's by a relative error of at most 0.0095.
Values may be sent and summed in bfloat16 or wider, within the bound.
A program may use at most 128 MiB of HBM per device.

```python
import math
import jax
import jax.numpy as jnp
from jax import lax

D = 4096
HEADS = 64
HEAD_DIM = 64
HD = 4096
ROWS = 8192
ENC = 8192


def draw_decoder_states(key, part):
    subkeys = jax.random.split(jax.random.fold_in(key, 11), 1)
    result = jnp.clip(jax.random.normal(subkeys[0], (ROWS, D), jnp.float32), -6.0, 6.0)
    return result.astype(jnp.bfloat16)


def draw_enc_keys(key, part):
    subkeys = jax.random.split(jax.random.fold_in(key, 23), 1)
    width = HEADS * HEAD_DIM
    result = jnp.clip(2.0 * jax.random.normal(subkeys[0], (ENC, width), jnp.float32), -8.0, 8.0)
    return result.astype(jnp.bfloat16)


def levels(own_key, dims, cuts, smallest, top_value):
    gain = 1.0
    for axis_at, parts in cuts:
        heights = jax.random.uniform(jax.random.fold_in(jax.random.fold_in(own_key, 6), axis_at), (parts,), jnp.float32, smallest / len(cuts), top_value / len(cuts))
        gain = gain * jnp.repeat(jnp.exp(heights), dims[axis_at] // parts).reshape((-1,) + (1,) * (len(dims) - 1 - axis_at))
    return gain


def noise(key, dims, scale, bound, cuts=(), held_as=jnp.bfloat16):
    values = scale * jax.random.normal(key, dims, jnp.float32)
    if cuts:
        values = values * levels(key, dims, cuts, -0.22, 0.18)
    return jnp.clip(values, -bound, bound).astype(held_as)


def setup_inputs(seed: int = 0) -> dict:
    key_list = jax.random.split(jax.random.key(seed), 6)
    return {
        "decoder_states": draw_decoder_states(jax.random.fold_in(key_list[5], 71), 0),
        "w_query": noise(key_list[1], (D, HD), D ** -0.5, 0.09375, ((0, 32), (1, 16))),
        "w_out_t": noise(key_list[2], (D, HD), (HD // 4) ** -0.5, 0.1875, ((0, 32), (1, 16))),
        "enc_keys": draw_enc_keys(jax.random.fold_in(key_list[5], 71), 0),
        "enc_values": noise(key_list[4], (ENC, HD), 1.0, 6.0, ((0, 32), (1, 16))),
    }


def reference(decoder_states, w_query, w_out_t, enc_keys, enc_values):
    queries = jnp.dot(decoder_states, w_query, preferred_element_type=jnp.float32).astype(jnp.bfloat16)
    factor = 1.0 / math.sqrt(HEAD_DIM)

    def one_head(head_index):
        offset = (head_index * HEAD_DIM).astype(jnp.int32)
        query_head = lax.dynamic_slice_in_dim(queries, offset, HEAD_DIM, 1)
        key_head = lax.dynamic_slice_in_dim(enc_keys, offset, HEAD_DIM, 1)
        value_head = lax.dynamic_slice_in_dim(enc_values, offset, HEAD_DIM, 1)
        scores = lax.dot_general(query_head, key_head, (((1,), (1,)), ((), ())), preferred_element_type=jnp.float32) * factor
        row_top = lax.optimization_barrier(jnp.max(scores, axis=1, keepdims=True))
        weights = jnp.exp(scores - row_top)
        row_sum = lax.optimization_barrier(jnp.sum(weights, axis=1, keepdims=True))
        blended = jnp.dot(weights.astype(jnp.bfloat16), value_head, preferred_element_type=jnp.float32)
        return (blended / row_sum).astype(jnp.bfloat16)
    context = lax.map(one_head, jnp.arange(HEADS, dtype=jnp.int32))
    context = jnp.transpose(context, (1, 0, 2)).reshape(ROWS, HEADS * HEAD_DIM)
    return lax.dot_general(context, w_out_t, (((1,), (1,)), ((), ())), preferred_element_type=jnp.float32).astype(jnp.bfloat16)
```

```python
import functools
import math

import jax
import jax.numpy as jnp
from jax import lax
from jax.experimental import pallas as pl
from jax.experimental.pallas import tpu as pltpu
from jax.sharding import PartitionSpec as P

HEAD_DIM = 64
NX, NY, NC, NZ, NH = 4, 4, 2, 8, 2
MESH = pl.DeviceIdType.MESH
BF16, F32 = jnp.bfloat16, jnp.float32
VMEM = pltpu.VMEM


def place():
    b = lax.axis_index("blk")
    f = lax.axis_index("fsdp")
    x = lax.div(b, NY * NC)
    y = lax.rem(lax.div(b, NC), NY)
    c = lax.rem(b, NC)
    return x, y, c, lax.div(f, NH), lax.rem(f, NH)


def blk_id(x, y, c):
    return {"blk": x * (NY * NC) + y * NC + c}


def fsdp_id(z, h):
    return {"fsdp": z * NH + h}


def greet(peers):
    barrier = pltpu.get_barrier_semaphore()
    for peer in peers:
        pl.semaphore_signal(barrier, inc=1, device_id=peer, device_id_type=MESH)
    pl.semaphore_wait(barrier, len(peers))


class Links:
    def __init__(self, send_sem, recv_sem):
        self.send_sem, self.recv_sem, self.copies = send_sem, recv_sem, []

    def send(self, src, dst, peer):
        k = len(self.copies)
        copy = pltpu.make_async_remote_copy(
            src_ref=src, dst_ref=dst, send_sem=self.send_sem.at[k],
            recv_sem=self.recv_sem.at[k], device_id=peer, device_id_type=MESH,
        )
        copy.start()
        self.copies.append(copy)
        return copy

    def drain(self):
        for copy in self.copies:
            copy.wait_send()


def gather_kernel(x_ref, wq_ref, wo_ref, kv_ref, xg, wqg, wog, kvg, local_sem, send_sem, recv_sem):
    x, y, c, z, h = place()
    xr, xl = lax.rem(x + 1, NX), lax.rem(x + NX - 1, NX)
    zr, zl = lax.rem(z + 1, NZ), lax.rem(z + NZ - 1, NZ)
    ys = [lax.rem(y + r, NY) for r in (1, 2, 3)]
    right, left, other = blk_id(xr, y, c), blk_id(xl, y, c), blk_id(x, y, 1 - c)
    up, down, far = fsdp_id(zr, h), fsdp_id(zl, h), fsdp_id(z, 1 - h)
    greet([right, left, other, up, down, far] + [blk_id(x, yp, c) for yp in ys])
    net = Links(send_sem, recv_sem)

    own = [
        pltpu.make_async_copy(x_ref, xg.at[z, h], local_sem.at[0]),
        pltpu.make_async_copy(wq_ref, wqg.at[x, y, c], local_sem.at[1]),
        pltpu.make_async_copy(kv_ref.at[y], kvg.at[x, y, c], local_sem.at[2]),
        pltpu.make_async_copy(wo_ref, wog.at[x, y, c], local_sem.at[3]),
    ]
    for copy in own:
        copy.start()
    pair = net.send(x_ref, xg.at[z, h], far)
    columns = []
    for buf, piece in ((wqg, lambda yp: wq_ref), (kvg, lambda yp: kv_ref.at[yp]), (wog, lambda yp: wo_ref)):
        columns.append([net.send(piece(yp), buf.at[x, y, c], blk_id(x, yp, c)) for yp in ys])
    for copy in own:
        copy.wait()

    def z_step(s):
        a, b = lax.rem(z + NZ - s, NZ), lax.rem(z + s, NZ)
        if s < 3:
            return (net.send(xg.at[a], xg.at[a], up), net.send(xg.at[b], xg.at[b], down))
        return (net.send(xg.at[a, 0], xg.at[a, 0], up), net.send(xg.at[b, 1], xg.at[b, 1], down))

    def x_first(buf, arrivals):
        for copy in arrivals:
            copy.wait_recv()
        block = buf.at[x, :, c]
        return (net.send(block, block, right), net.send(block, block, left))

    def x_second(buf, arrivals):
        for copy in arrivals:
            copy.wait_recv()
        a, b = buf.at[xl, pl.ds(0, 2), c], buf.at[xr, pl.ds(2, 2), c]
        return (net.send(a, a, right), net.send(b, b, left))

    def core_step(buf, arrivals):
        for copy in arrivals:
            copy.wait_recv()
        half = buf.at[:, :, c]
        return net.send(half, half, other)

    def z_wait(arrivals):
        for copy in arrivals:
            copy.wait_recv()

    bufs = (wqg, kvg, wog)
    pair.wait_recv()
    zc = z_step(0)
    first = [x_first(buf, got) for buf, got in zip(bufs, columns)]
    z_wait(zc)
    zc = z_step(1)
    second = [x_second(wqg, first[0])]
    z_wait(zc)
    zc = z_step(2)
    last = [core_step(wqg, second[0])]
    second.append(x_second(kvg, first[1]))
    z_wait(zc)
    zc = z_step(3)
    last.append(core_step(kvg, second[1]))
    second.append(x_second(wog, first[2]))
    last.append(core_step(wog, second[2]))
    z_wait(zc)
    z_wait(last)
    net.drain()


def gather(x, wq, wo, kv):
    rows, cols = x.shape
    depth = wq.shape[0]
    copies = 1 + 9 + 8 + 12 + 3
    any_spec = pl.BlockSpec(memory_space=pl.ANY)
    return pl.pallas_call(
        gather_kernel,
        name="gather_inputs",
        out_shape=(
            jax.ShapeDtypeStruct((NZ, NH, rows, cols), BF16),
            jax.ShapeDtypeStruct((NX, NY, NC, depth, cols), BF16),
            jax.ShapeDtypeStruct((NX, NY, NC, depth, cols), BF16),
            jax.ShapeDtypeStruct((NX, NY, NC) + kv.shape[1:], BF16),
        ),
        in_specs=[pl.BlockSpec(memory_space=VMEM)] * 4,
        out_specs=(any_spec,) * 4,
        scratch_shapes=[
            pltpu.SemaphoreType.DMA((4,)),
            pltpu.SemaphoreType.DMA((copies,)),
            pltpu.SemaphoreType.DMA((copies,)),
        ],
        compiler_params=pltpu.CompilerParams(collective_id=0, has_side_effects=True),
    )(x, wq, wo, kv)


def swap_kernel(src, dst, local_sem, send_sem, recv_sem):
    x, y, c, z, h = place()
    ys = [lax.rem(y + r, NY) for r in (1, 2, 3)]
    peers = [blk_id(x, yp, c) for yp in ys]
    greet(peers)
    net = Links(send_sem, recv_sem)
    own = pltpu.make_async_copy(src.at[y], dst.at[y], local_sem)
    own.start()
    got = [net.send(src.at[yp], dst.at[y], peer) for yp, peer in zip(ys, peers)]
    own.wait()
    for copy in got:
        copy.wait_recv()
    net.drain()


def swap(blocks, name, collective_id):
    return pl.pallas_call(
        swap_kernel,
        name=name,
        out_shape=jax.ShapeDtypeStruct(blocks.shape, blocks.dtype),
        in_specs=[pl.BlockSpec(memory_space=VMEM)],
        out_specs=pl.BlockSpec(memory_space=VMEM),
        scratch_shapes=[
            pltpu.SemaphoreType.DMA,
            pltpu.SemaphoreType.DMA((3,)),
            pltpu.SemaphoreType.DMA((3,)),
        ],
        compiler_params=pltpu.CompilerParams(collective_id=collective_id, has_side_effects=True),
    )(blocks)


def query_kernel(x_ref, w_ref, q_ref, total):
    step = pl.program_id(0)

    @pl.when(step == 0)
    def _():
        total[...] = jnp.zeros_like(total)

    for k in range(x_ref.shape[0]):
        total[...] += jnp.dot(x_ref[k], w_ref[k], preferred_element_type=F32)

    @pl.when(step == pl.num_programs(0) - 1)
    def _():
        q = total[...].astype(BF16)
        zero = jnp.zeros((q.shape[0], HEAD_DIM), BF16)
        for j in range(q_ref.shape[0]):
            q_ref[j] = jnp.concatenate([q[:, j * HEAD_DIM:(j + 1) * HEAD_DIM], zero], axis=1)


def project_queries(xg, wq):
    parts, rows, cols = xg.shape
    n = wq.shape[2]
    heads = n // HEAD_DIM
    return pl.pallas_call(
        query_kernel,
        name="project_queries",
        grid=(4,),
        out_shape=jax.ShapeDtypeStruct((heads, rows, 2 * HEAD_DIM), BF16),
        in_specs=[
            pl.BlockSpec((parts // 4, rows, cols), lambda i: (i, 0, 0)),
            pl.BlockSpec((parts // 4, cols, n), lambda i: (i, 0, 0)),
        ],
        out_specs=pl.BlockSpec((heads, rows, 2 * HEAD_DIM), lambda i: (0, 0, 0)),
        scratch_shapes=[VMEM((rows, n), F32)],
    )(xg, wq)


def attend_kernel(q_ref, kv_ref, o_ref, ones_v):
    keys = kv_ref.shape[0]
    chunk = 1024
    factor = 1.0 / (math.sqrt(HEAD_DIM) * math.log(2.0))

    @pl.when(pl.program_id(0) == 0)
    def _():
        lane = lax.broadcasted_iota(jnp.int32, (chunk, 2 * HEAD_DIM), 1)

        @pl.loop(0, keys // chunk)
        def _(i):
            at = pl.ds(pl.multiple_of(i * chunk, chunk), chunk)
            v = kv_ref[at, :].astype(F32)
            ones_v[at, :] = jnp.where(lane < HEAD_DIM, 1.0, v).astype(BF16)

    q = q_ref[...]
    rows = q.shape[0]

    def body(i, state):
        top, total = state
        at = pl.ds(pl.multiple_of(i * chunk, chunk), chunk)
        s = lax.dot_general(
            q, kv_ref[at, :], (((1,), (1,)), ((), ())), preferred_element_type=F32
        )
        new_top = jnp.maximum(top, jnp.max(s, axis=1, keepdims=True))
        p = jnp.exp2((s - new_top) * factor)
        rescale = jnp.exp2((top - new_top) * factor)
        total = total * rescale + jnp.dot(
            p.astype(BF16), ones_v[at, :], preferred_element_type=F32
        )
        return new_top, total

    start = (jnp.full((rows, 1), -jnp.inf, F32), jnp.zeros((rows, 2 * HEAD_DIM), F32))
    _, total = lax.fori_loop(0, keys // chunk, body, start, unroll=2)
    context = total[:, HEAD_DIM:] / total[:, :HEAD_DIM]
    o_ref[...] = jnp.concatenate([context, context], axis=1).astype(BF16)


def attend(q, kv):
    rows, wide = q.shape
    tile = 256
    return pl.pallas_call(
        attend_kernel,
        name="attend",
        grid=(rows // tile,),
        out_shape=jax.ShapeDtypeStruct((rows, wide), BF16),
        in_specs=[
            pl.BlockSpec((tile, wide), lambda i: (i, 0)),
            pl.BlockSpec(kv.shape, lambda i: (0, 0)),
        ],
        out_specs=pl.BlockSpec((tile, wide), lambda i: (i, 0)),
        scratch_shapes=[VMEM(kv.shape, BF16)],
    )(q, kv)


def project_kernel(c_ref, w_ref, o_ref):
    context = jnp.concatenate([c_ref[j][:, :HEAD_DIM] for j in range(c_ref.shape[0])], axis=1)
    o_ref[...] = lax.dot_general(
        context, w_ref[...], (((1,), (1,)), ((), ())), preferred_element_type=F32
    ).astype(BF16)


def project_out(context, wo):
    heads, rows, wide = context.shape
    out, cols = wo.shape
    tile = 1024
    return pl.pallas_call(
        project_kernel,
        name="project_out",
        grid=(out // tile,),
        out_shape=jax.ShapeDtypeStruct((rows, out), BF16),
        in_specs=[
            pl.BlockSpec((heads, rows, wide), lambda i: (0, 0, 0)),
            pl.BlockSpec((tile, cols), lambda i: (i, 0)),
        ],
        out_specs=pl.BlockSpec((rows, tile), lambda i: (0, i)),
    )(context, wo)


def reduce_kernel(p_ref, o_ref, half_r, half_l, in_r, in_l, out_r, out_l, total, far_out, far_in,
                  send_sem, recv_sem):
    x, y, c, z, h = place()
    up, down = fsdp_id(lax.rem(z + 1, NZ), h), fsdp_id(lax.rem(z + NZ - 1, NZ), h)
    far = fsdp_id(z, 1 - h)
    greet([up, down, far])
    net = Links(send_sem, recv_sem)
    opposite = lax.rem(z + 4, NZ)
    r = net.send(p_ref.at[opposite, 0], half_r, up)
    l = net.send(p_ref.at[opposite, 1], half_l, down)
    for s in range(3):
        ahead, behind = lax.rem(z + 3 - s, NZ), lax.rem(z + NZ - 3 + s, NZ)
        r.wait_recv()
        if s == 0:
            out_r[0, 0] = (p_ref[ahead, 0].astype(F32) + half_r[...].astype(F32)).astype(BF16)
            out_r[0, 1] = p_ref[ahead, 1]
        else:
            out_r[s] = (p_ref[ahead].astype(F32) + in_r[s - 1].astype(F32)).astype(BF16)
        r = net.send(out_r.at[s], in_r.at[s], up)
        l.wait_recv()
        if s == 0:
            out_l[0, 0] = p_ref[behind, 0]
            out_l[0, 1] = (p_ref[behind, 1].astype(F32) + half_l[...].astype(F32)).astype(BF16)
        else:
            out_l[s] = (p_ref[behind].astype(F32) + in_l[s - 1].astype(F32)).astype(BF16)
        l = net.send(out_l.at[s], in_l.at[s], down)
    r.wait_recv()
    l.wait_recv()
    total[...] = p_ref[z].astype(F32) + in_r[2].astype(F32) + in_l[2].astype(F32)
    far_out[...] = total[1 - h].astype(BF16)
    w = net.send(far_out, far_in, far)
    w.wait_recv()
    o_ref[...] = (total[h] + far_in[...].astype(F32)).astype(BF16)
    net.drain()


def reduce_rows(partial):
    one = partial.shape[2:]
    two = partial.shape[1:]
    return pl.pallas_call(
        reduce_kernel,
        name="reduce_rows",
        out_shape=jax.ShapeDtypeStruct(one, BF16),
        in_specs=[pl.BlockSpec(memory_space=VMEM)],
        out_specs=pl.BlockSpec(memory_space=VMEM),
        scratch_shapes=[
            VMEM(one, BF16), VMEM(one, BF16),
            VMEM((3,) + two, BF16), VMEM((3,) + two, BF16),
            VMEM((3,) + two, BF16), VMEM((3,) + two, BF16),
            VMEM(two, F32), VMEM(one, BF16), VMEM(one, BF16),
            pltpu.SemaphoreType.DMA((9,)),
            pltpu.SemaphoreType.DMA((9,)),
        ],
        compiler_params=pltpu.CompilerParams(collective_id=3, has_side_effects=True),
    )(partial)


def shards(decoder_states, w_query, w_out_t, enc_keys, enc_values):
    rows, cols = decoder_states.shape
    heads = cols // HEAD_DIM
    keys = enc_keys.reshape(-1, heads, HEAD_DIM)
    values = enc_values.reshape(-1, heads, HEAD_DIM)
    kv = jnp.transpose(jnp.concatenate([keys, values], axis=2), (1, 0, 2))
    xg, wqg, wog, kvg = gather(decoder_states, w_query, w_out_t, kv)
    q = project_queries(xg.reshape(NZ * NH, rows, cols), wqg.reshape(NZ * NH, cols, cols))
    q = swap(q, "swap_queries", 1)
    context = attend(q.reshape(NY * rows, 2 * HEAD_DIM), kvg.reshape(-1, 2 * HEAD_DIM))
    context = swap(context.reshape(NY, rows, 2 * HEAD_DIM), "swap_context", 2)
    partial = project_out(context, wog.reshape(-1, cols))
    return reduce_rows(partial.reshape(NZ, NH, rows // (NZ * NH), partial.shape[1]))


def solution(mesh):
    spec = P("blk", "fsdp")
    return jax.shard_map(
        shards, mesh=mesh, in_specs=(spec,) * 5,
        out_specs=P(("blk", "fsdp"), None), check_vma=False,
    )
```

```python
import math

import jax
import jax.numpy as jnp
from jax import lax
from jax.experimental import pallas as pl
from jax.experimental.pallas import tpu as pltpu
from jax.sharding import PartitionSpec as P

HEAD_DIM = 64
NX, NY, NC, NZ, NH = 4, 4, 2, 8, 2
MESH = pl.DeviceIdType.MESH
BF16, F32 = jnp.bfloat16, jnp.float32
VMEM = pltpu.VMEM


def place():
    b = lax.axis_index("blk")
    f = lax.axis_index("fsdp")
    x = lax.div(b, NY * NC)
    y = lax.rem(lax.div(b, NC), NY)
    c = lax.rem(b, NC)
    return x, y, c, lax.div(f, NH), lax.rem(f, NH)


def blk_id(x, y, c):
    return {"blk": x * (NY * NC) + y * NC + c}


def fsdp_id(z, h):
    return {"fsdp": z * NH + h}


def greet(peers):
    barrier = pltpu.get_barrier_semaphore()
    for peer in peers:
        pl.semaphore_signal(barrier, inc=1, device_id=peer, device_id_type=MESH)
    return lambda: pl.semaphore_wait(barrier, len(peers))


def arrive(copies):
    for copy in copies:
        copy.wait_recv()


class Links:
    def __init__(self, send_sem, recv_sem):
        self.send_sem, self.recv_sem, self.copies = send_sem, recv_sem, []

    def send(self, src, dst, peer):
        k = len(self.copies)
        copy = pltpu.make_async_remote_copy(
            src_ref=src, dst_ref=dst, send_sem=self.send_sem.at[k],
            recv_sem=self.recv_sem.at[k], device_id=peer, device_id_type=MESH,
        )
        copy.start()
        self.copies.append(copy)
        return copy

    def drain(self):
        for copy in self.copies:
            copy.wait_send()


class Spread:
    def __init__(self, net, buf, x, y, c):
        self.net, self.buf, self.c, self.x = net, buf, c, x
        self.xs = [lax.rem(x + r, NX) for r in (1, 2, 3)]
        self.right, self.left = blk_id(self.xs[0], y, c), blk_id(self.xs[2], y, c)
        self.other = blk_id(x, y, 1 - c)
        self.cores = []

    def to_core(self, *xs):
        for at in xs:
            block = self.buf.at[at, :, self.c]
            self.cores.append(self.net.send(block, block, self.other))

    def first(self, arrivals):
        arrive(arrivals)
        block = self.buf.at[self.x, :, self.c]
        self.hop = (self.net.send(block, block, self.right), self.net.send(block, block, self.left))
        self.to_core(self.x)

    def second(self):
        arrive(self.hop)
        a = self.buf.at[self.xs[2], pl.ds(0, 2), self.c]
        b = self.buf.at[self.xs[0], pl.ds(2, 2), self.c]
        self.hop = (self.net.send(a, a, self.right), self.net.send(b, b, self.left))
        self.to_core(self.xs[0], self.xs[2])

    def third(self):
        arrive(self.hop)
        self.to_core(self.xs[1])

    def finish(self):
        arrive(self.cores)


def queries_kernel(x_ref, wq_ref, k_ref, v_ref, q_ref, kvg, xg, wqg, kv, qs, local_sem, send_sem, recv_sem):
    x, y, c, z, h = place()
    ys = [lax.rem(y + r, NY) for r in (1, 2, 3)]
    column = [blk_id(x, yp, c) for yp in ys]
    up, down = fsdp_id(lax.rem(z + 1, NZ), h), fsdp_id(lax.rem(z + NZ - 1, NZ), h)
    far = fsdp_id(z, 1 - h)
    net = Links(send_sem, recv_sem)
    weights, pairs = Spread(net, wqg, x, y, c), Spread(net, kvg, x, y, c)
    ready = greet([weights.right, weights.left, weights.other, up, down, far] + column)
    for j in range(NY):
        cols = slice(j * HEAD_DIM, (j + 1) * HEAD_DIM)
        kv[j] = jnp.concatenate([k_ref[:, cols], v_ref[:, cols]], axis=1)
    ready()

    def ring(s, part, is_own, both):
        a, b = lax.rem(z + NZ - s, NZ), lax.rem(z + s, NZ)
        sent = []
        if both != "down":
            src = x_ref if is_own and s == 0 else xg.at[a, part]
            sent.append(net.send(src, xg.at[a, part], up))
        if both != "up":
            src = x_ref if is_own and s == 0 else xg.at[b, part]
            sent.append(net.send(src, xg.at[b, part], down))
        return sent

    pair = net.send(x_ref, xg.at[z, h], far)
    own_ring = ring(0, h, True, "both")
    own = [
        pltpu.make_async_copy(x_ref, xg.at[z, h], local_sem.at[0]),
        pltpu.make_async_copy(wq_ref, wqg.at[x, y, c], local_sem.at[1]),
        pltpu.make_async_copy(kv.at[y], kvg.at[x, y, c], local_sem.at[2]),
    ]
    for copy in own:
        copy.start()
    w_col = [net.send(wq_ref, wqg.at[x, y, c], to) for to in column]
    kv_col = [net.send(kv.at[yp], kvg.at[x, y, c], to) for yp, to in zip(ys, column)]
    for copy in own:
        copy.wait()
    arrive(own_ring)
    own_ring = ring(1, h, True, "both")
    weights.first(w_col)
    arrive(own_ring)
    own_ring = ring(2, h, True, "both")
    arrive([pair])
    far_ring = ring(0, 1 - h, False, "both")
    pairs.first(kv_col)
    arrive(own_ring)
    own_ring = ring(3, h, True, "up")
    weights.second()
    arrive(far_ring)
    far_ring = ring(1, 1 - h, False, "both")
    weights.third()
    pairs.second()
    arrive(far_ring)
    far_ring = ring(2, 1 - h, False, "both")
    pairs.third()
    arrive(own_ring)
    arrive(far_ring)
    far_ring = ring(3, 1 - h, False, "down")
    weights.finish()
    arrive(far_ring)

    total = None
    for f in range(NZ * NH):
        w = wqg[f // NY, f % NY]
        part = jnp.dot(
            xg[f // NH, f % NH], w.reshape(-1, w.shape[-1]), preferred_element_type=F32
        )
        total = part if total is None else total + part
    q = total.astype(BF16)
    zero = jnp.zeros((q.shape[0], HEAD_DIM), BF16)
    for j in range(NY):
        qs[j] = jnp.concatenate([q[:, j * HEAD_DIM:(j + 1) * HEAD_DIM], zero], axis=1)
    swaps = [net.send(qs.at[yp], q_ref.at[y], to) for yp, to in zip(ys, column)]
    q_ref[y] = qs[y]
    pairs.finish()
    arrive(swaps)
    net.drain()


def queries_and_pairs(x, wq, k, v):
    rows, cols = x.shape
    depth = wq.shape[0]
    heads = (NY, rows, 2 * HEAD_DIM)
    vmem = pl.BlockSpec(memory_space=VMEM)
    return pl.pallas_call(
        queries_kernel,
        name="queries_and_pairs",
        out_shape=(
            jax.ShapeDtypeStruct(heads, BF16),
            jax.ShapeDtypeStruct((NX, NY, NC, rows, 2 * HEAD_DIM), BF16),
        ),
        in_specs=[vmem] * 4,
        out_specs=(vmem, pl.BlockSpec(memory_space=pl.ANY)),
        scratch_shapes=[
            VMEM((NZ, NH, rows, cols), BF16),
            VMEM((NX, NY, NC, depth, cols), BF16),
            VMEM(heads, BF16),
            VMEM(heads, BF16),
            pltpu.SemaphoreType.DMA((3,)),
            pltpu.SemaphoreType.DMA((40,)),
            pltpu.SemaphoreType.DMA((40,)),
        ],
        compiler_params=pltpu.CompilerParams(collective_id=0, has_side_effects=True),
    )(x, wq, k, v)


def attend_kernel(q_ref, kv_ref, wo_ref, o_ref, wog, ones_v, done, local_sem, send_sem, recv_sem):
    x, y, c, z, h = place()
    ys = [lax.rem(y + r, NY) for r in (1, 2, 3)]
    column = [blk_id(x, yp, c) for yp in ys]
    net = Links(send_sem, recv_sem)
    weights = Spread(net, wog, x, y, c)
    ready = greet([weights.right, weights.left, weights.other] + column)
    keys = kv_ref.shape[0]
    chunk = 1024
    factor = 1.0 / (math.sqrt(HEAD_DIM) * math.log(2.0))

    lane = lax.broadcasted_iota(jnp.int32, (chunk, 2 * HEAD_DIM), 1)

    @pl.loop(0, keys // chunk)
    def _(i):
        at = pl.ds(pl.multiple_of(i * chunk, chunk), chunk)
        v = kv_ref[at, :].astype(F32)
        ones_v[at, :] = jnp.where(lane < HEAD_DIM, 1.0, v).astype(BF16)

    def attend(tile):
        q = q_ref[tile]
        rows = q.shape[0]

        def body(i, state):
            top, total = state
            at = pl.ds(pl.multiple_of(i * chunk, chunk), chunk)
            s = lax.dot_general(
                q, kv_ref[at, :], (((1,), (1,)), ((), ())), preferred_element_type=F32
            )
            new_top = jnp.maximum(top, jnp.max(s, axis=1, keepdims=True))
            p = jnp.exp2((s - new_top) * factor)
            rescale = jnp.exp2((top - new_top) * factor)
            total = total * rescale + jnp.dot(
                p.astype(BF16), ones_v[at, :], preferred_element_type=F32
            )
            return new_top, total

        start = (jnp.full((rows, 1), -jnp.inf, F32), jnp.zeros((rows, 2 * HEAD_DIM), F32))
        _, total = lax.fori_loop(0, keys // chunk, body, start, unroll=2)
        context = total[:, HEAD_DIM:] / total[:, :HEAD_DIM]
        return jnp.concatenate([context, context], axis=1).astype(BF16)

    ready()
    own = pltpu.make_async_copy(wo_ref, wog.at[x, y, c], local_sem)
    own.start()
    w_col = [net.send(wo_ref, wog.at[x, y, c], to) for to in column]
    own.wait()
    swaps = []
    steps = [lambda: weights.first(w_col), weights.second, weights.third]
    for i, (yp, to) in enumerate(zip(ys, column)):
        done[i] = attend(yp)
        steps[i]()
        swaps.append(net.send(done.at[i], o_ref.at[y], to))
    o_ref[y] = attend(y)
    weights.finish()
    arrive(swaps)
    net.drain()


def attend(q, kv, wo):
    depth, cols = wo.shape
    vmem = pl.BlockSpec(memory_space=VMEM)
    return pl.pallas_call(
        attend_kernel,
        name="attend",
        out_shape=(
            jax.ShapeDtypeStruct(q.shape, BF16),
            jax.ShapeDtypeStruct((NX, NY, NC, depth, cols), BF16),
        ),
        in_specs=[vmem] * 3,
        out_specs=(vmem, pl.BlockSpec(memory_space=pl.ANY)),
        scratch_shapes=[
            VMEM(kv.shape, BF16),
            VMEM((3,) + q.shape[1:], BF16),
            pltpu.SemaphoreType.DMA,
            pltpu.SemaphoreType.DMA((14,)),
            pltpu.SemaphoreType.DMA((14,)),
        ],
        compiler_params=pltpu.CompilerParams(collective_id=1, has_side_effects=True),
    )(q, kv, wo)


CUTS = 2


def output_kernel(c_ref, w_ref, o_ref, p, half_r, half_l, in_r, in_l, out_r, out_l, total, far_out, far_in,
                  send_sem, recv_sem):
    x, y, c, z, h = place()
    up, down = fsdp_id(lax.rem(z + 1, NZ), h), fsdp_id(lax.rem(z + NZ - 1, NZ), h)
    far = fsdp_id(z, 1 - h)
    ready = greet([up, down, far])
    net = Links(send_sem, recv_sem)
    width = p.shape[-1]
    piece = 512
    context = jnp.concatenate([c_ref[j][:, :HEAD_DIM] for j in range(c_ref.shape[0])], axis=1)
    opposite = lax.rem(z + 4, NZ)
    rs, ls = [], []
    for k in range(CUTS):
        for i in range(width // piece):
            part = lax.dot_general(
                context, w_ref[pl.ds(k * width + i * piece, piece), :],
                (((1,), (1,)), ((), ())), preferred_element_type=F32,
            ).astype(BF16)
            p[k, :, :, :, pl.ds(i * piece, piece)] = part.reshape(p.shape[1:4] + (piece,))
        if k == 0:
            ready()
        rs.append(net.send(p.at[k, opposite, 0], half_r.at[k], up))
        ls.append(net.send(p.at[k, opposite, 1], half_l.at[k], down))
    for s in range(3):
        ahead, behind = lax.rem(z + 3 - s, NZ), lax.rem(z + NZ - 3 + s, NZ)
        for k in range(CUTS):
            arrive([rs[k]])
            if s == 0:
                out_r[k, 0, 0] = (p[k, ahead, 0].astype(F32) + half_r[k].astype(F32)).astype(BF16)
                out_r[k, 0, 1] = p[k, ahead, 1]
            else:
                out_r[k, s] = (p[k, ahead].astype(F32) + in_r[k, s - 1].astype(F32)).astype(BF16)
            rs[k] = net.send(out_r.at[k, s], in_r.at[k, s], up)
            arrive([ls[k]])
            if s == 0:
                out_l[k, 0, 0] = p[k, behind, 0]
                out_l[k, 0, 1] = (p[k, behind, 1].astype(F32) + half_l[k].astype(F32)).astype(BF16)
            else:
                out_l[k, s] = (p[k, behind].astype(F32) + in_l[k, s - 1].astype(F32)).astype(BF16)
            ls[k] = net.send(out_l.at[k, s], in_l.at[k, s], down)
    fars = []
    for k in range(CUTS):
        arrive([rs[k], ls[k]])
        total[k] = p[k, z].astype(F32) + in_r[k, 2].astype(F32) + in_l[k, 2].astype(F32)
        far_out[k] = total[k, 1 - h].astype(BF16)
        fars.append(net.send(far_out.at[k], far_in.at[k], far))
    for k in range(CUTS):
        arrive([fars[k]])
        o_ref[:, pl.ds(k * width, width)] = (total[k, h] + far_in[k].astype(F32)).astype(BF16)
    net.drain()


def project_and_reduce(context, wo):
    rows, out = context.shape[1], wo.shape[0]
    mine = rows // (NZ * NH)
    one = (CUTS, mine, out // CUTS)
    two = (CUTS, NH, mine, out // CUTS)
    chain = (CUTS, 3, NH, mine, out // CUTS)
    vmem = pl.BlockSpec(memory_space=VMEM)
    return pl.pallas_call(
        output_kernel,
        name="project_and_reduce",
        out_shape=jax.ShapeDtypeStruct((mine, out), BF16),
        in_specs=[vmem] * 2,
        out_specs=vmem,
        scratch_shapes=[
            VMEM((CUTS, NZ, NH, mine, out // CUTS), BF16),
            VMEM(one, BF16), VMEM(one, BF16),
            VMEM(chain, BF16), VMEM(chain, BF16), VMEM(chain, BF16), VMEM(chain, BF16),
            VMEM(two, F32), VMEM(one, BF16), VMEM(one, BF16),
            pltpu.SemaphoreType.DMA((9 * CUTS,)),
            pltpu.SemaphoreType.DMA((9 * CUTS,)),
        ],
        compiler_params=pltpu.CompilerParams(collective_id=2, has_side_effects=True),
    )(context, wo)


def shards(decoder_states, w_query, w_out_t, enc_keys, enc_values):
    cols = w_out_t.shape[1]
    q, kv = queries_and_pairs(decoder_states, w_query, enc_keys, enc_values)
    context, wo = attend(q, kv.reshape(-1, 2 * HEAD_DIM), w_out_t)
    return project_and_reduce(context, wo.reshape(-1, cols))


def solution(mesh):
    spec = P("blk", "fsdp")
    return jax.shard_map(
        shards, mesh=mesh, in_specs=(spec,) * 5,
        out_specs=P(("blk", "fsdp"), None), check_vma=False,
    )
```

```python
import math

import jax
import jax.numpy as jnp
from jax import lax
from jax.experimental import pallas as pl
from jax.experimental.pallas import tpu as pltpu
from jax.sharding import PartitionSpec as P

HEAD_DIM = 64
NX, NY, NC, NZ, NH = 4, 4, 2, 8, 2
MESH = pl.DeviceIdType.MESH
BF16, F32 = jnp.bfloat16, jnp.float32
VMEM = pltpu.VMEM


def place():
    b = lax.axis_index("blk")
    f = lax.axis_index("fsdp")
    x = lax.div(b, NY * NC)
    y = lax.rem(lax.div(b, NC), NY)
    c = lax.rem(b, NC)
    return x, y, c, lax.div(f, NH), lax.rem(f, NH)


def blk_id(x, y, c):
    return {"blk": x * (NY * NC) + y * NC + c}


def fsdp_id(z, h):
    return {"fsdp": z * NH + h}


def greet(peers):
    barrier = pltpu.get_barrier_semaphore()
    for peer in peers:
        pl.semaphore_signal(barrier, inc=1, device_id=peer, device_id_type=MESH)
    return lambda: pl.semaphore_wait(barrier, len(peers))


def arrive(copies):
    for copy in copies:
        copy.wait_recv()


class Links:
    def __init__(self, send_sem, recv_sem):
        self.send_sem, self.recv_sem, self.copies = send_sem, recv_sem, []

    def send(self, src, dst, peer):
        k = len(self.copies)
        copy = pltpu.make_async_remote_copy(
            src_ref=src, dst_ref=dst, send_sem=self.send_sem.at[k],
            recv_sem=self.recv_sem.at[k], device_id=peer, device_id_type=MESH,
        )
        copy.start()
        self.copies.append(copy)
        return copy

    def drain(self):
        for copy in self.copies:
            copy.wait_send()


class Spread:
    def __init__(self, net, buf, x, y, c):
        self.net, self.buf, self.c, self.x = net, buf, c, x
        self.xs = [lax.rem(x + r, NX) for r in (1, 2, 3)]
        self.ys = [lax.rem(y + r, NY) for r in range(NY)]
        self.right, self.left = blk_id(self.xs[0], y, c), blk_id(self.xs[2], y, c)
        self.other = blk_id(x, y, 1 - c)
        self.column = [blk_id(x, yp, c) for yp in self.ys]
        self.hops, self.halves, self.cores = [None] * NY, [None] * NY, []

    def spread_y(self, pieces):
        at = self.buf.at[self.x, self.ys[0], self.c]
        self.got = [
            self.net.send(piece, at, to) for piece, to in zip(pieces[1:], self.column[1:])
        ]

    def first(self, r, piece=None):
        at = self.buf.at[self.x, self.ys[r], self.c]
        if r > 0:
            arrive([self.got[NY - 1 - r]])
        src = at if piece is None else piece
        self.hops[r] = (self.net.send(src, at, self.right), self.net.send(src, at, self.left))

    def second(self, r):
        arrive(self.hops[r])
        if r < 2:
            at = self.buf.at[self.xs[2], self.ys[r], self.c]
            self.halves[r] = self.net.send(at, at, self.right)
        else:
            at = self.buf.at[self.xs[0], self.ys[r], self.c]
            self.halves[r] = self.net.send(at, at, self.left)

    def to_core(self, *xs):
        for at in xs:
            block = self.buf.at[at, :, self.c]
            self.cores.append(self.net.send(block, block, self.other))

    def core_own(self):
        self.to_core(self.x)

    def core_near(self):
        self.to_core(self.xs[0], self.xs[2])

    def core_far(self):
        arrive(self.halves)
        self.to_core(self.xs[1])

    def finish(self):
        arrive(self.cores)


def queries_kernel(x_ref, wq_ref, k_ref, v_ref, q_ref, kvg, xg, wqg, kv, qs, local_sem, send_sem, recv_sem):
    x, y, c, z, h = place()
    ys = [lax.rem(y + r, NY) for r in (1, 2, 3)]
    column = [blk_id(x, yp, c) for yp in ys]
    up, down = fsdp_id(lax.rem(z + 1, NZ), h), fsdp_id(lax.rem(z + NZ - 1, NZ), h)
    far = fsdp_id(z, 1 - h)
    net = Links(send_sem, recv_sem)
    weights, pairs = Spread(net, wqg, x, y, c), Spread(net, kvg, x, y, c)
    ready = greet([weights.right, weights.left, weights.other, up, down, far] + column)
    for j in range(NY):
        cols = slice(j * HEAD_DIM, (j + 1) * HEAD_DIM)
        kv[j] = jnp.concatenate([k_ref[:, cols], v_ref[:, cols]], axis=1)
    ready()
    steps = []

    def at_time(when, step, *args):
        steps.append((when, len(steps), lambda: step(*args)))

    def ring(key, s, part, first_row, count, is_own, ways):
        if s > 0:
            arrive(rings[key])
        row = pl.ds(first_row, count)
        sent = []
        for way, to, slot in (("up", up, lax.rem(z + NZ - s, NZ)), ("down", down, lax.rem(z + s, NZ))):
            if way in ways:
                at = xg.at[slot, part, row]
                sent.append(net.send(x_ref.at[row] if is_own and s == 0 else at, at, to))
        rings[key] = sent

    rings = {}
    both = ("up", "down")
    rows = x_ref.shape[0]
    for j in range(2):
        for s in range(4):
            at_time(4 * s + j, ring, ("own", j), s, h, j * (rows // 2), rows // 2, True, both if s < 3 else ("up",))
    pair = []
    quarter = rows // 4
    for j in range(4):
        row = pl.ds(j * quarter, quarter)
        pair.append(net.send(x_ref.at[row], xg.at[z, h, row], far))

        def start(j=j):
            arrive([pair[j]])
            ring(("far", j), 0, 1 - h, j * quarter, quarter, False, both)

        base = 6.5 + 1.7 * j
        at_time(base, start)
        for s in range(1, 4):
            at_time(base + 3.8 * s, ring, ("far", j), s, 1 - h, j * quarter, quarter, False,
                    both if s < 3 else ("down",))
    own = [
        pltpu.make_async_copy(x_ref, xg.at[z, h], local_sem.at[0]),
        pltpu.make_async_copy(wq_ref, wqg.at[x, y, c], local_sem.at[1]),
        pltpu.make_async_copy(kv.at[y], kvg.at[x, y, c], local_sem.at[2]),
    ]
    for copy in own:
        copy.start()

    def own_done():
        for copy in own:
            copy.wait()

    at_time(3.2, own_done)
    at_time(0.1, weights.spread_y, [wq_ref] * NY)
    at_time(0.2, weights.first, 0, wq_ref)
    at_time(3.5, pairs.spread_y, [kv.at[yp] for yp in pairs.ys])
    at_time(3.6, pairs.first, 0, kv.at[y])
    for unit, base in ((weights, 6.0), (pairs, 14.0)):
        for k, r in enumerate((3, 2, 1)):
            at_time(base + 1.7 * k, unit.first, r)
        at_time(base + 0.5, unit.second, 0)
        for k, r in enumerate((3, 2, 1)):
            at_time(base + 6 + 1.7 * k, unit.second, r)
        at_time(base + 3.6, unit.core_own)
        at_time(base + 9.6, unit.core_near)
        at_time(base + 13, unit.core_far)
    for _, _, step in sorted(steps, key=lambda item: item[:2]):
        step()
    for sent in rings.values():
        arrive(sent)
    weights.finish()

    total = None
    for f in range(NZ * NH):
        w = wqg[f // NY, f % NY]
        part = jnp.dot(
            xg[f // NH, f % NH], w.reshape(-1, w.shape[-1]), preferred_element_type=F32
        )
        total = part if total is None else total + part
    q = total.astype(BF16)
    zero = jnp.zeros((q.shape[0], HEAD_DIM), BF16)
    for j in range(NY):
        qs[j] = jnp.concatenate([q[:, j * HEAD_DIM:(j + 1) * HEAD_DIM], zero], axis=1)
    swaps = [net.send(qs.at[yp], q_ref.at[y], to) for yp, to in zip(ys, column)]
    q_ref[y] = qs[y]
    pairs.finish()
    arrive(swaps)
    net.drain()


def queries_and_pairs(x, wq, k, v):
    rows, cols = x.shape
    depth = wq.shape[0]
    heads = (NY, rows, 2 * HEAD_DIM)
    vmem = pl.BlockSpec(memory_space=VMEM)
    return pl.pallas_call(
        queries_kernel,
        name="queries_and_pairs",
        out_shape=(
            jax.ShapeDtypeStruct(heads, BF16),
            jax.ShapeDtypeStruct((NX, NY, NC, rows, 2 * HEAD_DIM), BF16),
        ),
        in_specs=[vmem] * 4,
        out_specs=(vmem, pl.BlockSpec(memory_space=pl.ANY)),
        scratch_shapes=[
            VMEM((NZ, NH, rows, cols), BF16),
            VMEM((NX, NY, NC, depth, cols), BF16),
            VMEM(heads, BF16),
            VMEM(heads, BF16),
            pltpu.SemaphoreType.DMA((3,)),
            pltpu.SemaphoreType.DMA((88,)),
            pltpu.SemaphoreType.DMA((88,)),
        ],
        compiler_params=pltpu.CompilerParams(collective_id=0, has_side_effects=True),
    )(x, wq, k, v)


def attend_kernel(q_ref, kv_ref, wo_ref, o_ref, wog, ones_v, done, local_sem, send_sem, recv_sem):
    x, y, c, z, h = place()
    ys = [lax.rem(y + r, NY) for r in (1, 2, 3)]
    column = [blk_id(x, yp, c) for yp in ys]
    net = Links(send_sem, recv_sem)
    weights = Spread(net, wog, x, y, c)
    ready = greet([weights.right, weights.left, weights.other] + column)
    keys = kv_ref.shape[0]
    chunk = 1024
    factor = 1.0 / (math.sqrt(HEAD_DIM) * math.log(2.0))

    lane = lax.broadcasted_iota(jnp.int32, (chunk, 2 * HEAD_DIM), 1)

    @pl.loop(0, keys // chunk)
    def _(i):
        at = pl.ds(pl.multiple_of(i * chunk, chunk), chunk)
        v = kv_ref[at, :].astype(F32)
        ones_v[at, :] = jnp.where(lane < HEAD_DIM, 1.0, v).astype(BF16)

    def attend(tile):
        q = q_ref[tile]
        rows = q.shape[0]

        def body(i, state):
            top, total = state
            at = pl.ds(pl.multiple_of(i * chunk, chunk), chunk)
            s = lax.dot_general(
                q, kv_ref[at, :], (((1,), (1,)), ((), ())), preferred_element_type=F32
            )
            new_top = jnp.maximum(top, jnp.max(s, axis=1, keepdims=True))
            p = jnp.exp2((s - new_top) * factor)
            rescale = jnp.exp2((top - new_top) * factor)
            total = total * rescale + jnp.dot(
                p.astype(BF16), ones_v[at, :], preferred_element_type=F32
            )
            return new_top, total

        start = (jnp.full((rows, 1), -jnp.inf, F32), jnp.zeros((rows, 2 * HEAD_DIM), F32))
        _, total = lax.fori_loop(0, keys // chunk, body, start, unroll=4)
        context = total[:, HEAD_DIM:] / total[:, :HEAD_DIM]
        return jnp.concatenate([context, context], axis=1).astype(BF16)

    ready()
    own = pltpu.make_async_copy(wo_ref, wog.at[x, y, c], local_sem)
    own.start()
    weights.spread_y([wo_ref] * NY)
    weights.first(0, wo_ref)
    own.wait()
    swaps = []

    def near():
        for r in (3, 2, 1):
            weights.first(r)
        weights.core_own()
        weights.second(0)

    def across():
        for r in (3, 2, 1):
            weights.second(r)
        weights.core_near()

    steps = [near, across, weights.core_far]
    for i, (yp, to) in enumerate(zip(ys, column)):
        done[i] = attend(yp)
        steps[i]()
        swaps.append(net.send(done.at[i], o_ref.at[y], to))
    o_ref[y] = attend(y)
    weights.finish()
    arrive(swaps)
    net.drain()


def attend(q, kv, wo):
    depth, cols = wo.shape
    vmem = pl.BlockSpec(memory_space=VMEM)
    return pl.pallas_call(
        attend_kernel,
        name="attend",
        out_shape=(
            jax.ShapeDtypeStruct(q.shape, BF16),
            jax.ShapeDtypeStruct((NX, NY, NC, depth, cols), BF16),
        ),
        in_specs=[vmem] * 3,
        out_specs=(vmem, pl.BlockSpec(memory_space=pl.ANY)),
        scratch_shapes=[
            VMEM(kv.shape, BF16),
            VMEM((3,) + q.shape[1:], BF16),
            pltpu.SemaphoreType.DMA,
            pltpu.SemaphoreType.DMA((22,)),
            pltpu.SemaphoreType.DMA((22,)),
        ],
        compiler_params=pltpu.CompilerParams(collective_id=1, has_side_effects=True),
    )(q, kv, wo)


CUTS = 4


def output_kernel(c_ref, w_ref, o_ref, p, half_r, half_l, in_r, in_l, out_r, out_l, total, far_out, far_in,
                  send_sem, recv_sem):
    x, y, c, z, h = place()
    up, down = fsdp_id(lax.rem(z + 1, NZ), h), fsdp_id(lax.rem(z + NZ - 1, NZ), h)
    far = fsdp_id(z, 1 - h)
    ready = greet([up, down, far])
    net = Links(send_sem, recv_sem)
    width = p.shape[-1]
    piece = 512
    context = jnp.concatenate([c_ref[j][:, :HEAD_DIM] for j in range(c_ref.shape[0])], axis=1)
    opposite = lax.rem(z + 4, NZ)
    rs, ls = [], []
    for k in range(CUTS):
        for i in range(width // piece):
            part = lax.dot_general(
                context, w_ref[pl.ds(k * width + i * piece, piece), :],
                (((1,), (1,)), ((), ())), preferred_element_type=F32,
            ).astype(BF16)
            p[k, :, :, :, pl.ds(i * piece, piece)] = part.reshape(p.shape[1:4] + (piece,))
        if k == 0:
            ready()
        rs.append(net.send(p.at[k, opposite, 0], half_r.at[k], up))
        ls.append(net.send(p.at[k, opposite, 1], half_l.at[k], down))
    for s in range(3):
        ahead, behind = lax.rem(z + 3 - s, NZ), lax.rem(z + NZ - 3 + s, NZ)
        for k in range(CUTS):
            arrive([rs[k]])
            if s == 0:
                out_r[k, 0, 0] = (p[k, ahead, 0].astype(F32) + half_r[k].astype(F32)).astype(BF16)
                out_r[k, 0, 1] = p[k, ahead, 1]
            else:
                out_r[k, s] = (p[k, ahead].astype(F32) + in_r[k, s - 1].astype(F32)).astype(BF16)
            rs[k] = net.send(out_r.at[k, s], in_r.at[k, s], up)
            arrive([ls[k]])
            if s == 0:
                out_l[k, 0, 0] = p[k, behind, 0]
                out_l[k, 0, 1] = (p[k, behind, 1].astype(F32) + half_l[k].astype(F32)).astype(BF16)
            else:
                out_l[k, s] = (p[k, behind].astype(F32) + in_l[k, s - 1].astype(F32)).astype(BF16)
            ls[k] = net.send(out_l.at[k, s], in_l.at[k, s], down)
    fars = []
    for k in range(CUTS):
        arrive([rs[k], ls[k]])
        total[k] = p[k, z].astype(F32) + in_r[k, 2].astype(F32) + in_l[k, 2].astype(F32)
        far_out[k] = total[k, 1 - h].astype(BF16)
        fars.append(net.send(far_out.at[k], far_in.at[k], far))
    for k in range(CUTS):
        arrive([fars[k]])
        o_ref[:, pl.ds(k * width, width)] = (total[k, h] + far_in[k].astype(F32)).astype(BF16)
    net.drain()


def project_and_reduce(context, wo):
    rows, out = context.shape[1], wo.shape[0]
    mine = rows // (NZ * NH)
    one = (CUTS, mine, out // CUTS)
    two = (CUTS, NH, mine, out // CUTS)
    chain = (CUTS, 3, NH, mine, out // CUTS)
    vmem = pl.BlockSpec(memory_space=VMEM)
    return pl.pallas_call(
        output_kernel,
        name="project_and_reduce",
        out_shape=jax.ShapeDtypeStruct((mine, out), BF16),
        in_specs=[vmem] * 2,
        out_specs=vmem,
        scratch_shapes=[
            VMEM((CUTS, NZ, NH, mine, out // CUTS), BF16),
            VMEM(one, BF16), VMEM(one, BF16),
            VMEM(chain, BF16), VMEM(chain, BF16), VMEM(chain, BF16), VMEM(chain, BF16),
            VMEM(two, F32), VMEM(one, BF16), VMEM(one, BF16),
            pltpu.SemaphoreType.DMA((9 * CUTS,)),
            pltpu.SemaphoreType.DMA((9 * CUTS,)),
        ],
        compiler_params=pltpu.CompilerParams(collective_id=2, has_side_effects=True),
    )(context, wo)


def shards(decoder_states, w_query, w_out_t, enc_keys, enc_values):
    cols = w_out_t.shape[1]
    q, kv = queries_and_pairs(decoder_states, w_query, enc_keys, enc_values)
    context, wo = attend(q, kv.reshape(-1, 2 * HEAD_DIM), w_out_t)
    return project_and_reduce(context, wo.reshape(-1, cols))


def solution(mesh):
    spec = P("blk", "fsdp")
    return jax.shard_map(
        shards, mesh=mesh, in_specs=(spec,) * 5,
        out_specs=P(("blk", "fsdp"), None), check_vma=False,
    )
```

```python
import math

import jax
import jax.numpy as jnp
from jax import lax
from jax.experimental import pallas as pl
from jax.experimental.pallas import tpu as pltpu
from jax.sharding import PartitionSpec as P

HEAD_DIM = 64
NX, NY, NC, NZ, NH = 4, 4, 2, 8, 2
MESH = pl.DeviceIdType.MESH
BF16, F32 = jnp.bfloat16, jnp.float32
VMEM = pltpu.VMEM


def place():
    b = lax.axis_index("blk")
    f = lax.axis_index("fsdp")
    x = lax.div(b, NY * NC)
    y = lax.rem(lax.div(b, NC), NY)
    c = lax.rem(b, NC)
    return x, y, c, lax.div(f, NH), lax.rem(f, NH)


def blk_id(x, y, c):
    return {"blk": x * (NY * NC) + y * NC + c}


def fsdp_id(z, h):
    return {"fsdp": z * NH + h}


def greet(peers):
    barrier = pltpu.get_barrier_semaphore()
    for peer in peers:
        pl.semaphore_signal(barrier, inc=1, device_id=peer, device_id_type=MESH)
    return lambda: pl.semaphore_wait(barrier, len(peers))


def arrive(copies):
    for copy in copies:
        copy.wait_recv()


class Links:
    def __init__(self, send_sem, recv_sem):
        self.send_sem, self.recv_sem, self.copies = send_sem, recv_sem, []

    def send(self, src, dst, peer):
        k = len(self.copies)
        copy = pltpu.make_async_remote_copy(
            src_ref=src, dst_ref=dst, send_sem=self.send_sem.at[k],
            recv_sem=self.recv_sem.at[k], device_id=peer, device_id_type=MESH,
        )
        copy.start()
        self.copies.append(copy)
        return copy

    def drain(self):
        for copy in self.copies:
            copy.wait_send()


class Spread:
    def __init__(self, net, buf, x, y, c):
        self.net, self.buf, self.c, self.x = net, buf, c, x
        self.xs = [lax.rem(x + r, NX) for r in (1, 2, 3)]
        self.ys = [lax.rem(y + r, NY) for r in range(NY)]
        self.right, self.left = blk_id(self.xs[0], y, c), blk_id(self.xs[2], y, c)
        self.other = blk_id(x, y, 1 - c)
        self.column = [blk_id(x, yp, c) for yp in self.ys]
        self.hops, self.halves, self.cores = [None] * NY, [None] * NY, []

    def spread_y(self, pieces):
        at = self.buf.at[self.x, self.ys[0], self.c]
        self.got = [
            self.net.send(piece, at, to) for piece, to in zip(pieces[1:], self.column[1:])
        ]

    def first(self, r, piece=None):
        at = self.buf.at[self.x, self.ys[r], self.c]
        if r > 0:
            arrive([self.got[NY - 1 - r]])
        src = at if piece is None else piece
        self.hops[r] = (self.net.send(src, at, self.right), self.net.send(src, at, self.left))

    def second(self, r):
        arrive(self.hops[r])
        if r < 2:
            at = self.buf.at[self.xs[2], self.ys[r], self.c]
            self.halves[r] = self.net.send(at, at, self.right)
        else:
            at = self.buf.at[self.xs[0], self.ys[r], self.c]
            self.halves[r] = self.net.send(at, at, self.left)

    def to_core(self, *xs):
        for at in xs:
            block = self.buf.at[at, :, self.c]
            self.cores.append(self.net.send(block, block, self.other))

    def core_own(self):
        self.to_core(self.x)

    def core_near(self):
        self.to_core(self.xs[0], self.xs[2])

    def core_far(self):
        arrive(self.halves)
        self.to_core(self.xs[1])

    def finish(self):
        arrive(self.cores)


def queries_kernel(x_ref, wq_ref, k_ref, v_ref, q_ref, kvg, xg, wqg, kv, qs, local_sem, send_sem, recv_sem):
    x, y, c, z, h = place()
    ys = [lax.rem(y + r, NY) for r in (1, 2, 3)]
    column = [blk_id(x, yp, c) for yp in ys]
    up, down = fsdp_id(lax.rem(z + 1, NZ), h), fsdp_id(lax.rem(z + NZ - 1, NZ), h)
    far = fsdp_id(z, 1 - h)
    net = Links(send_sem, recv_sem)
    weights, pairs = Spread(net, wqg, x, y, c), Spread(net, kvg, x, y, c)
    ready = greet([weights.right, weights.left, weights.other, up, down, far] + column)
    for j in range(NY):
        cols = slice(j * HEAD_DIM, (j + 1) * HEAD_DIM)
        kv[j] = jnp.concatenate([k_ref[:, cols], v_ref[:, cols]], axis=1)
    ready()
    steps = []

    def at_time(when, step, *args):
        steps.append((when, len(steps), lambda: step(*args)))

    def ring(key, s, part, first_row, count, is_own, ways):
        if s > 0:
            arrive(rings[key])
        row = pl.ds(first_row, count)
        sent = []
        for way, to, slot in (("up", up, lax.rem(z + NZ - s, NZ)), ("down", down, lax.rem(z + s, NZ))):
            if way in ways:
                at = xg.at[slot, part, row]
                sent.append(net.send(x_ref.at[row] if is_own and s == 0 else at, at, to))
        rings[key] = sent

    rings = {}
    both = ("up", "down")
    rows = x_ref.shape[0]
    for j in range(2):
        for s in range(4):
            at_time(4 * s + j, ring, ("own", j), s, h, j * (rows // 2), rows // 2, True, both if s < 3 else ("up",))
    pair = []
    quarter = rows // 4
    for j in range(4):
        row = pl.ds(j * quarter, quarter)
        pair.append(net.send(x_ref.at[row], xg.at[z, h, row], far))

        def start(j=j):
            arrive([pair[j]])
            ring(("far", j), 0, 1 - h, j * quarter, quarter, False, both)

        base = 6.5 + 1.7 * j
        at_time(base, start)
        for s in range(1, 4):
            at_time(base + 3.8 * s, ring, ("far", j), s, 1 - h, j * quarter, quarter, False,
                    both if s < 3 else ("down",))
    own = [
        pltpu.make_async_copy(x_ref, xg.at[z, h], local_sem.at[0]),
        pltpu.make_async_copy(wq_ref, wqg.at[x, y, c], local_sem.at[1]),
        pltpu.make_async_copy(kv.at[y], kvg.at[x, y, c], local_sem.at[2]),
    ]
    for copy in own:
        copy.start()

    def own_done():
        for copy in own:
            copy.wait()

    at_time(3.2, own_done)
    at_time(4.2, weights.spread_y, [wq_ref] * NY)
    at_time(0.2, weights.first, 0, wq_ref)
    at_time(11.5, pairs.spread_y, [kv.at[yp] for yp in pairs.ys])
    at_time(3.6, pairs.first, 0, kv.at[y])
    for unit, base in ((weights, 10.5), (pairs, 19.0)):
        for k, r in enumerate((3, 2, 1)):
            at_time(base + 1.7 * k, unit.first, r)
        at_time(base + 0.5, unit.second, 0)
        for k, r in enumerate((3, 2, 1)):
            at_time(base + 6 + 1.7 * k, unit.second, r)
        at_time(base + 3.6, unit.core_own)
        at_time(base + 9.6, unit.core_near)
        at_time(base + 13, unit.core_far)
    for _, _, step in sorted(steps, key=lambda item: item[:2]):
        step()
    for sent in rings.values():
        arrive(sent)
    weights.finish()

    total = None
    for f in range(NZ * NH):
        w = wqg[f // NY, f % NY]
        part = jnp.dot(
            xg[f // NH, f % NH], w.reshape(-1, w.shape[-1]), preferred_element_type=F32
        )
        total = part if total is None else total + part
    q = total.astype(BF16)
    for j in range(NY):
        head = q[:, j * HEAD_DIM:(j + 1) * HEAD_DIM]
        qs[j] = jnp.concatenate([head[:rows // 2], head[rows // 2:]], axis=1)
    swaps = [net.send(qs.at[yp], q_ref.at[y], to) for yp, to in zip(ys, column)]
    q_ref[y] = qs[y]
    pairs.finish()
    arrive(swaps)
    net.drain()


def queries_and_pairs(x, wq, k, v):
    rows, cols = x.shape
    depth = wq.shape[0]
    heads = (NY, rows, 2 * HEAD_DIM)
    packed = (NY, rows // 2, 2 * HEAD_DIM)
    vmem = pl.BlockSpec(memory_space=VMEM)
    return pl.pallas_call(
        queries_kernel,
        name="queries_and_pairs",
        out_shape=(
            jax.ShapeDtypeStruct(packed, BF16),
            jax.ShapeDtypeStruct((NX, NY, NC, rows, 2 * HEAD_DIM), BF16),
        ),
        in_specs=[vmem] * 4,
        out_specs=(vmem, pl.BlockSpec(memory_space=pl.ANY)),
        scratch_shapes=[
            VMEM((NZ, NH, rows, cols), BF16),
            VMEM((NX, NY, NC, depth, cols), BF16),
            VMEM(heads, BF16),
            VMEM(packed, BF16),
            pltpu.SemaphoreType.DMA((3,)),
            pltpu.SemaphoreType.DMA((88,)),
            pltpu.SemaphoreType.DMA((88,)),
        ],
        compiler_params=pltpu.CompilerParams(collective_id=0, has_side_effects=True),
    )(x, wq, k, v)


def attend_kernel(q_ref, kv_ref, wo_ref, o_ref, wog, ones_v, done, local_sem, send_sem, recv_sem):
    x, y, c, z, h = place()
    ys = [lax.rem(y + r, NY) for r in (1, 2, 3)]
    column = [blk_id(x, yp, c) for yp in ys]
    net = Links(send_sem, recv_sem)
    weights = Spread(net, wog, x, y, c)
    ready = greet([weights.right, weights.left, weights.other] + column)
    keys = kv_ref.shape[0]
    chunk = 2048
    factor = 1.0 / (math.sqrt(HEAD_DIM) * math.log(2.0))

    lane = lax.broadcasted_iota(jnp.int32, (chunk, 2 * HEAD_DIM), 1)

    @pl.loop(0, keys // chunk)
    def _(i):
        at = pl.ds(pl.multiple_of(i * chunk, chunk), chunk)
        v = kv_ref[at, :].astype(F32)
        ones_v[at, :] = jnp.where(lane < HEAD_DIM, 1.0, v).astype(BF16)

    def attend(tile):
        two = q_ref[tile]
        zero = jnp.zeros((two.shape[0], HEAD_DIM), BF16)
        q = jnp.concatenate([
            jnp.concatenate([two[:, :HEAD_DIM], zero], axis=1),
            jnp.concatenate([two[:, HEAD_DIM:], zero], axis=1),
        ], axis=0)
        rows = q.shape[0]

        def body(i, state):
            top, total = state
            at = pl.ds(pl.multiple_of(i * chunk, chunk), chunk)
            s = lax.dot_general(
                q, kv_ref[at, :], (((1,), (1,)), ((), ())), preferred_element_type=F32
            )
            new_top = jnp.maximum(top, jnp.max(s, axis=1, keepdims=True))
            p = jnp.exp2((s - new_top) * factor)
            rescale = jnp.exp2((top - new_top) * factor)
            total = total * rescale + jnp.dot(
                p.astype(BF16), ones_v[at, :], preferred_element_type=F32
            )
            return new_top, total

        start = (jnp.full((rows, 1), -jnp.inf, F32), jnp.zeros((rows, 2 * HEAD_DIM), F32))
        _, total = lax.fori_loop(0, keys // chunk, body, start, unroll=4)
        context = total[:, HEAD_DIM:] / total[:, :HEAD_DIM]
        return jnp.concatenate([context, context], axis=1).astype(BF16)

    ready()
    own = pltpu.make_async_copy(wo_ref, wog.at[x, y, c], local_sem)
    own.start()
    weights.spread_y([wo_ref] * NY)
    weights.first(0, wo_ref)
    own.wait()
    swaps = []

    def near():
        for r in (3, 2, 1):
            weights.first(r)
        weights.core_own()
        weights.second(0)

    def across():
        for r in (3, 2, 1):
            weights.second(r)
        weights.core_near()

    steps = [near, across, weights.core_far]
    for i, (yp, to) in enumerate(zip(ys, column)):
        done[i] = attend(yp)
        steps[i]()
        swaps.append(net.send(done.at[i], o_ref.at[y], to))
    o_ref[y] = attend(y)
    weights.finish()
    arrive(swaps)
    net.drain()


def attend(q, kv, wo):
    depth, cols = wo.shape
    context = (q.shape[0], 2 * q.shape[1], q.shape[2])
    vmem = pl.BlockSpec(memory_space=VMEM)
    return pl.pallas_call(
        attend_kernel,
        name="attend",
        out_shape=(
            jax.ShapeDtypeStruct(context, BF16),
            jax.ShapeDtypeStruct((NX, NY, NC, depth, cols), BF16),
        ),
        in_specs=[vmem] * 3,
        out_specs=(vmem, pl.BlockSpec(memory_space=pl.ANY)),
        scratch_shapes=[
            VMEM(kv.shape, BF16),
            VMEM((3,) + context[1:], BF16),
            pltpu.SemaphoreType.DMA,
            pltpu.SemaphoreType.DMA((22,)),
            pltpu.SemaphoreType.DMA((22,)),
        ],
        compiler_params=pltpu.CompilerParams(collective_id=1, has_side_effects=True),
    )(q, kv, wo)


CUTS = 4


def output_kernel(c_ref, w_ref, o_ref, p, half_r, half_l, in_r, in_l, out_r, out_l, total, far_out, far_in,
                  send_sem, recv_sem):
    x, y, c, z, h = place()
    up, down = fsdp_id(lax.rem(z + 1, NZ), h), fsdp_id(lax.rem(z + NZ - 1, NZ), h)
    far = fsdp_id(z, 1 - h)
    ready = greet([up, down, far])
    net = Links(send_sem, recv_sem)
    width = p.shape[-1]
    piece = 512
    context = jnp.concatenate([c_ref[j][:, :HEAD_DIM] for j in range(c_ref.shape[0])], axis=1)
    opposite = lax.rem(z + 4, NZ)
    rs, ls = [], []
    for k in range(CUTS):
        for i in range(width // piece):
            part = lax.dot_general(
                context, w_ref[pl.ds(k * width + i * piece, piece), :],
                (((1,), (1,)), ((), ())), preferred_element_type=F32,
            ).astype(BF16)
            p[k, :, :, :, pl.ds(i * piece, piece)] = part.reshape(p.shape[1:4] + (piece,))
        if k == 0:
            ready()
        rs.append(net.send(p.at[k, opposite, 0], half_r.at[k], up))
        ls.append(net.send(p.at[k, opposite, 1], half_l.at[k], down))
    for s in range(3):
        ahead, behind = lax.rem(z + 3 - s, NZ), lax.rem(z + NZ - 3 + s, NZ)
        for k in range(CUTS):
            arrive([rs[k]])
            if s == 0:
                out_r[k, 0, 0] = (p[k, ahead, 0].astype(F32) + half_r[k].astype(F32)).astype(BF16)
                out_r[k, 0, 1] = p[k, ahead, 1]
            else:
                out_r[k, s] = (p[k, ahead].astype(F32) + in_r[k, s - 1].astype(F32)).astype(BF16)
            rs[k] = net.send(out_r.at[k, s], in_r.at[k, s], up)
            arrive([ls[k]])
            if s == 0:
                out_l[k, 0, 0] = p[k, behind, 0]
                out_l[k, 0, 1] = (p[k, behind, 1].astype(F32) + half_l[k].astype(F32)).astype(BF16)
            else:
                out_l[k, s] = (p[k, behind].astype(F32) + in_l[k, s - 1].astype(F32)).astype(BF16)
            ls[k] = net.send(out_l.at[k, s], in_l.at[k, s], down)
    fars = []
    for k in range(CUTS):
        arrive([rs[k], ls[k]])
        total[k] = p[k, z].astype(F32) + in_r[k, 2].astype(F32) + in_l[k, 2].astype(F32)
        far_out[k] = total[k, 1 - h].astype(BF16)
        fars.append(net.send(far_out.at[k], far_in.at[k], far))
    for k in range(CUTS):
        arrive([fars[k]])
        o_ref[:, pl.ds(k * width, width)] = (total[k, h] + far_in[k].astype(F32)).astype(BF16)
    net.drain()


def project_and_reduce(context, wo):
    rows, out = context.shape[1], wo.shape[0]
    mine = rows // (NZ * NH)
    one = (CUTS, mine, out // CUTS)
    two = (CUTS, NH, mine, out // CUTS)
    chain = (CUTS, 3, NH, mine, out // CUTS)
    vmem = pl.BlockSpec(memory_space=VMEM)
    return pl.pallas_call(
        output_kernel,
        name="project_and_reduce",
        out_shape=jax.ShapeDtypeStruct((mine, out), BF16),
        in_specs=[vmem] * 2,
        out_specs=vmem,
        scratch_shapes=[
            VMEM((CUTS, NZ, NH, mine, out // CUTS), BF16),
            VMEM(one, BF16), VMEM(one, BF16),
            VMEM(chain, BF16), VMEM(chain, BF16), VMEM(chain, BF16), VMEM(chain, BF16),
            VMEM(two, F32), VMEM(one, BF16), VMEM(one, BF16),
            pltpu.SemaphoreType.DMA((9 * CUTS,)),
            pltpu.SemaphoreType.DMA((9 * CUTS,)),
        ],
        compiler_params=pltpu.CompilerParams(collective_id=2, has_side_effects=True),
    )(context, wo)


def shards(decoder_states, w_query, w_out_t, enc_keys, enc_values):
    cols = w_out_t.shape[1]
    q, kv = queries_and_pairs(decoder_states, w_query, enc_keys, enc_values)
    context, wo = attend(q, kv.reshape(-1, 2 * HEAD_DIM), w_out_t)
    return project_and_reduce(context, wo.reshape(-1, cols))


def solution(mesh):
    spec = P("blk", "fsdp")
    return jax.shard_map(
        shards, mesh=mesh, in_specs=(spec,) * 5,
        out_specs=P(("blk", "fsdp"), None), check_vma=False,
    )
```

```python
import math

import jax
import jax.numpy as jnp
from jax import lax
from jax.experimental import pallas as pl
from jax.experimental.pallas import tpu as pltpu
from jax.sharding import PartitionSpec as P

HEAD_DIM = 64
NX, NY, NC, NZ, NH = 4, 4, 2, 8, 2
MESH = pl.DeviceIdType.MESH
BF16, F32 = jnp.bfloat16, jnp.float32
VMEM = pltpu.VMEM


def place():
    b = lax.axis_index("blk")
    f = lax.axis_index("fsdp")
    x = lax.div(b, NY * NC)
    y = lax.rem(lax.div(b, NC), NY)
    c = lax.rem(b, NC)
    return x, y, c, lax.div(f, NH), lax.rem(f, NH)


def blk_id(x, y, c):
    return {"blk": x * (NY * NC) + y * NC + c}


def fsdp_id(z, h):
    return {"fsdp": z * NH + h}


def greet(peers):
    barrier = pltpu.get_barrier_semaphore()
    for peer in peers:
        pl.semaphore_signal(barrier, inc=1, device_id=peer, device_id_type=MESH)
    return lambda: pl.semaphore_wait(barrier, len(peers))


def arrive(copies):
    for copy in copies:
        copy.wait_recv()


class Links:
    def __init__(self, send_sem, recv_sem):
        self.send_sem, self.recv_sem, self.copies = send_sem, recv_sem, []

    def send(self, src, dst, peer):
        k = len(self.copies)
        copy = pltpu.make_async_remote_copy(
            src_ref=src, dst_ref=dst, send_sem=self.send_sem.at[k],
            recv_sem=self.recv_sem.at[k], device_id=peer, device_id_type=MESH,
        )
        copy.start()
        self.copies.append(copy)
        return copy

    def drain(self):
        for copy in self.copies:
            copy.wait_send()


class Spread:
    def __init__(self, net, buf, x, y, c):
        self.net, self.buf, self.c, self.x = net, buf, c, x
        self.xs = [lax.rem(x + r, NX) for r in (1, 2, 3)]
        self.ys = [lax.rem(y + r, NY) for r in range(NY)]
        self.right, self.left = blk_id(self.xs[0], y, c), blk_id(self.xs[2], y, c)
        self.other = blk_id(x, y, 1 - c)
        self.column = [blk_id(x, yp, c) for yp in self.ys]
        self.hops, self.halves, self.cores = [None] * NY, [None] * NY, []

    def spread_y(self, pieces):
        at = self.buf.at[self.x, self.ys[0], self.c]
        self.got = [
            self.net.send(piece, at, to) for piece, to in zip(pieces[1:], self.column[1:])
        ]

    def first(self, r, piece=None):
        at = self.buf.at[self.x, self.ys[r], self.c]
        if r > 0:
            arrive([self.got[NY - 1 - r]])
        src = at if piece is None else piece
        self.hops[r] = (self.net.send(src, at, self.right), self.net.send(src, at, self.left))

    def second(self, r):
        arrive(self.hops[r])
        if r < 2:
            at = self.buf.at[self.xs[2], self.ys[r], self.c]
            self.halves[r] = self.net.send(at, at, self.right)
        else:
            at = self.buf.at[self.xs[0], self.ys[r], self.c]
            self.halves[r] = self.net.send(at, at, self.left)

    def to_core(self, *xs):
        for at in xs:
            block = self.buf.at[at, :, self.c]
            self.cores.append(self.net.send(block, block, self.other))

    def core_own(self):
        self.to_core(self.x)

    def core_near(self):
        self.to_core(self.xs[0], self.xs[2])

    def core_far(self):
        arrive(self.halves)
        self.to_core(self.xs[1])

    def finish(self):
        arrive(self.cores)


def queries_kernel(x_ref, wq_ref, k_ref, v_ref, q_ref, kvg, xg, wqg, kv, qs, local_sem, send_sem, recv_sem):
    x, y, c, z, h = place()
    ys = [lax.rem(y + r, NY) for r in (1, 2, 3)]
    column = [blk_id(x, yp, c) for yp in ys]
    up, down = fsdp_id(lax.rem(z + 1, NZ), h), fsdp_id(lax.rem(z + NZ - 1, NZ), h)
    far = fsdp_id(z, 1 - h)
    net = Links(send_sem, recv_sem)
    weights, pairs = Spread(net, wqg, x, y, c), Spread(net, kvg, x, y, c)
    ready = greet([weights.right, weights.left, weights.other, up, down, far] + column)
    for j in range(NY):
        cols = slice(j * HEAD_DIM, (j + 1) * HEAD_DIM)
        kv[j] = jnp.concatenate([k_ref[:, cols], v_ref[:, cols]], axis=1)
    ready()
    steps = []

    def at_time(when, step, *args):
        steps.append((when, len(steps), lambda: step(*args)))

    def ring(key, s, part, first_row, count, is_own, ways):
        if s > 0:
            arrive(rings[key])
        row = pl.ds(first_row, count)
        sent = []
        for way, to, slot in (("up", up, lax.rem(z + NZ - s, NZ)), ("down", down, lax.rem(z + s, NZ))):
            if way in ways:
                at = xg.at[slot, part, row]
                sent.append(net.send(x_ref.at[row] if is_own and s == 0 else at, at, to))
        rings[key] = sent

    rings = {}
    both = ("up", "down")
    rows = x_ref.shape[0]
    for j in range(2):
        for s in range(4):
            at_time(4 * s + j, ring, ("own", j), s, h, j * (rows // 2), rows // 2, True, both if s < 3 else ("up",))
    pair = []
    quarter = rows // 4
    for j in range(4):
        row = pl.ds(j * quarter, quarter)
        pair.append(net.send(x_ref.at[row], xg.at[z, h, row], far))

        def start(j=j):
            arrive([pair[j]])
            ring(("far", j), 0, 1 - h, j * quarter, quarter, False, both)

        base = 6.5 + 1.7 * j
        at_time(base, start)
        for s in range(1, 4):
            at_time(base + 3.8 * s, ring, ("far", j), s, 1 - h, j * quarter, quarter, False,
                    both if s < 3 else ("down",))
    own = [
        pltpu.make_async_copy(x_ref, xg.at[z, h], local_sem.at[0]),
        pltpu.make_async_copy(wq_ref, wqg.at[x, y, c], local_sem.at[1]),
        pltpu.make_async_copy(kv.at[y], kvg.at[x, y, c], local_sem.at[2]),
    ]
    for copy in own:
        copy.start()

    def own_done():
        for copy in own:
            copy.wait()

    at_time(3.2, own_done)
    at_time(5.5, weights.spread_y, [wq_ref] * NY)
    at_time(0.2, weights.first, 0, wq_ref)
    at_time(6.8, pairs.spread_y, [kv.at[yp] for yp in pairs.ys])
    at_time(3.6, pairs.first, 0, kv.at[y])
    for unit, base in ((weights, 11.5), (pairs, 15.0)):
        for k, r in enumerate((3, 2, 1)):
            at_time(base + 1.7 * k, unit.first, r)
        at_time(base + 0.5, unit.second, 0)
        for k, r in enumerate((3, 2, 1)):
            at_time(base + 6 + 1.7 * k, unit.second, r)
        at_time(base + 3.6, unit.core_own)
        at_time(base + 9.6, unit.core_near)
        at_time(base + 13, unit.core_far)
    for _, _, step in sorted(steps, key=lambda item: item[:2]):
        step()
    for sent in rings.values():
        arrive(sent)
    weights.finish()

    total = None
    for f in range(NZ * NH):
        w = wqg[f // NY, f % NY]
        part = jnp.dot(
            xg[f // NH, f % NH], w.reshape(-1, w.shape[-1]), preferred_element_type=F32
        )
        total = part if total is None else total + part
    q = total.astype(BF16)
    for j in range(NY):
        head = q[:, j * HEAD_DIM:(j + 1) * HEAD_DIM]
        qs[j] = jnp.concatenate([head[:rows // 2], head[rows // 2:]], axis=1)
    swaps = [net.send(qs.at[yp], q_ref.at[y], to) for yp, to in zip(ys, column)]
    q_ref[y] = qs[y]
    pairs.finish()
    arrive(swaps)
    net.drain()


def queries_and_pairs(x, wq, k, v):
    rows, cols = x.shape
    depth = wq.shape[0]
    heads = (NY, rows, 2 * HEAD_DIM)
    packed = (NY, rows // 2, 2 * HEAD_DIM)
    vmem = pl.BlockSpec(memory_space=VMEM)
    return pl.pallas_call(
        queries_kernel,
        name="queries_and_pairs",
        out_shape=(
            jax.ShapeDtypeStruct(packed, BF16),
            jax.ShapeDtypeStruct((NX, NY, NC, rows, 2 * HEAD_DIM), BF16),
        ),
        in_specs=[vmem] * 4,
        out_specs=(vmem, pl.BlockSpec(memory_space=pl.ANY)),
        scratch_shapes=[
            VMEM((NZ, NH, rows, cols), BF16),
            VMEM((NX, NY, NC, depth, cols), BF16),
            VMEM(heads, BF16),
            VMEM(packed, BF16),
            pltpu.SemaphoreType.DMA((3,)),
            pltpu.SemaphoreType.DMA((88,)),
            pltpu.SemaphoreType.DMA((88,)),
        ],
        compiler_params=pltpu.CompilerParams(collective_id=0, has_side_effects=True),
    )(x, wq, k, v)


def attend_kernel(q_ref, kv_ref, wo_ref, o_ref, wog, ones_v, done, local_sem, send_sem, recv_sem):
    x, y, c, z, h = place()
    ys = [lax.rem(y + r, NY) for r in (1, 2, 3)]
    column = [blk_id(x, yp, c) for yp in ys]
    net = Links(send_sem, recv_sem)
    weights = Spread(net, wog, x, y, c)
    ready = greet([weights.right, weights.left, weights.other] + column)
    keys = kv_ref.shape[0]
    chunk = 2048
    factor = 1.0 / (math.sqrt(HEAD_DIM) * math.log(2.0))

    lane = lax.broadcasted_iota(jnp.int32, (chunk, 2 * HEAD_DIM), 1)

    @pl.loop(0, keys // chunk)
    def _(i):
        at = pl.ds(pl.multiple_of(i * chunk, chunk), chunk)
        v = kv_ref[at, :].astype(F32)
        ones_v[at, :] = jnp.where(lane < HEAD_DIM, 1.0, v).astype(BF16)

    def attend(tile):
        two = q_ref[tile]
        zero = jnp.zeros((two.shape[0], HEAD_DIM), BF16)
        q = jnp.concatenate([
            jnp.concatenate([two[:, :HEAD_DIM], zero], axis=1),
            jnp.concatenate([two[:, HEAD_DIM:], zero], axis=1),
        ], axis=0)
        rows = q.shape[0]

        def body(i, state):
            top, total = state
            at = pl.ds(pl.multiple_of(i * chunk, chunk), chunk)
            s = lax.dot_general(
                q, kv_ref[at, :], (((1,), (1,)), ((), ())), preferred_element_type=F32
            )
            new_top = jnp.maximum(top, jnp.max(s, axis=1, keepdims=True))
            p = jnp.exp2((s - new_top) * factor)
            rescale = jnp.exp2((top - new_top) * factor)
            total = total * rescale + jnp.dot(
                p.astype(BF16), ones_v[at, :], preferred_element_type=F32
            )
            return new_top, total

        start = (jnp.full((rows, 1), -jnp.inf, F32), jnp.zeros((rows, 2 * HEAD_DIM), F32))
        _, total = lax.fori_loop(0, keys // chunk, body, start, unroll=4)
        context = total[:, HEAD_DIM:] / total[:, :HEAD_DIM]
        return jnp.concatenate([context, context], axis=1).astype(BF16)

    ready()
    own = pltpu.make_async_copy(wo_ref, wog.at[x, y, c], local_sem)
    own.start()
    weights.spread_y([wo_ref] * NY)
    weights.first(0, wo_ref)
    own.wait()
    swaps = []

    def near():
        for r in (3, 2, 1):
            weights.first(r)
        weights.core_own()
        weights.second(0)

    def across():
        for r in (3, 2, 1):
            weights.second(r)
        weights.core_near()

    steps = [near, across, weights.core_far]
    for i, (yp, to) in enumerate(zip(ys, column)):
        done[i] = attend(yp)
        steps[i]()
        swaps.append(net.send(done.at[i], o_ref.at[y], to))
    o_ref[y] = attend(y)
    weights.finish()
    arrive(swaps)
    net.drain()


def attend(q, kv, wo):
    depth, cols = wo.shape
    context = (q.shape[0], 2 * q.shape[1], q.shape[2])
    vmem = pl.BlockSpec(memory_space=VMEM)
    return pl.pallas_call(
        attend_kernel,
        name="attend",
        out_shape=(
            jax.ShapeDtypeStruct(context, BF16),
            jax.ShapeDtypeStruct((NX, NY, NC, depth, cols), BF16),
        ),
        in_specs=[vmem] * 3,
        out_specs=(vmem, pl.BlockSpec(memory_space=pl.ANY)),
        scratch_shapes=[
            VMEM(kv.shape, BF16),
            VMEM((3,) + context[1:], BF16),
            pltpu.SemaphoreType.DMA,
            pltpu.SemaphoreType.DMA((22,)),
            pltpu.SemaphoreType.DMA((22,)),
        ],
        compiler_params=pltpu.CompilerParams(collective_id=1, has_side_effects=True),
    )(q, kv, wo)


CUTS = 4


def output_kernel(c_ref, w_ref, o_ref, p, half_r, half_l, in_r, in_l, out_r, out_l, total, far_out, far_in,
                  send_sem, recv_sem):
    x, y, c, z, h = place()
    up, down = fsdp_id(lax.rem(z + 1, NZ), h), fsdp_id(lax.rem(z + NZ - 1, NZ), h)
    far = fsdp_id(z, 1 - h)
    ready = greet([up, down, far])
    net = Links(send_sem, recv_sem)
    width = p.shape[-1]
    piece = 512
    context = jnp.concatenate([c_ref[j][:, :HEAD_DIM] for j in range(c_ref.shape[0])], axis=1)
    opposite = lax.rem(z + 4, NZ)
    rs, ls = [], []
    for k in range(CUTS):
        for i in range(width // piece):
            part = lax.dot_general(
                context, w_ref[pl.ds(k * width + i * piece, piece), :],
                (((1,), (1,)), ((), ())), preferred_element_type=F32,
            ).astype(BF16)
            p[k, :, :, :, pl.ds(i * piece, piece)] = part.reshape(p.shape[1:4] + (piece,))
        if k == 0:
            ready()
        rs.append(net.send(p.at[k, opposite, 0], half_r.at[k], up))
        ls.append(net.send(p.at[k, opposite, 1], half_l.at[k], down))
    for s in range(3):
        ahead, behind = lax.rem(z + 3 - s, NZ), lax.rem(z + NZ - 3 + s, NZ)
        for k in range(CUTS):
            arrive([rs[k]])
            if s == 0:
                out_r[k, 0, 0] = (p[k, ahead, 0].astype(F32) + half_r[k].astype(F32)).astype(BF16)
                out_r[k, 0, 1] = p[k, ahead, 1]
            else:
                out_r[k, s] = (p[k, ahead].astype(F32) + in_r[k, s - 1].astype(F32)).astype(BF16)
            rs[k] = net.send(out_r.at[k, s], in_r.at[k, s], up)
            arrive([ls[k]])
            if s == 0:
                out_l[k, 0, 0] = p[k, behind, 0]
                out_l[k, 0, 1] = (p[k, behind, 1].astype(F32) + half_l[k].astype(F32)).astype(BF16)
            else:
                out_l[k, s] = (p[k, behind].astype(F32) + in_l[k, s - 1].astype(F32)).astype(BF16)
            ls[k] = net.send(out_l.at[k, s], in_l.at[k, s], down)
    fars = []
    for k in range(CUTS):
        arrive([rs[k], ls[k]])
        total[k] = p[k, z].astype(F32) + in_r[k, 2].astype(F32) + in_l[k, 2].astype(F32)
        far_out[k] = total[k, 1 - h].astype(BF16)
        fars.append(net.send(far_out.at[k], far_in.at[k], far))
    for k in range(CUTS):
        arrive([fars[k]])
        o_ref[:, pl.ds(k * width, width)] = (total[k, h] + far_in[k].astype(F32)).astype(BF16)
    net.drain()


def project_and_reduce(context, wo):
    rows, out = context.shape[1], wo.shape[0]
    mine = rows // (NZ * NH)
    one = (CUTS, mine, out // CUTS)
    two = (CUTS, NH, mine, out // CUTS)
    chain = (CUTS, 3, NH, mine, out // CUTS)
    vmem = pl.BlockSpec(memory_space=VMEM)
    return pl.pallas_call(
        output_kernel,
        name="project_and_reduce",
        out_shape=jax.ShapeDtypeStruct((mine, out), BF16),
        in_specs=[vmem] * 2,
        out_specs=vmem,
        scratch_shapes=[
            VMEM((CUTS, NZ, NH, mine, out // CUTS), BF16),
            VMEM(one, BF16), VMEM(one, BF16),
            VMEM(chain, BF16), VMEM(chain, BF16), VMEM(chain, BF16), VMEM(chain, BF16),
            VMEM(two, F32), VMEM(one, BF16), VMEM(one, BF16),
            pltpu.SemaphoreType.DMA((9 * CUTS,)),
            pltpu.SemaphoreType.DMA((9 * CUTS,)),
        ],
        compiler_params=pltpu.CompilerParams(collective_id=2, has_side_effects=True),
    )(context, wo)


def shards(decoder_states, w_query, w_out_t, enc_keys, enc_values):
    cols = w_out_t.shape[1]
    q, kv = queries_and_pairs(decoder_states, w_query, enc_keys, enc_values)
    context, wo = attend(q, kv.reshape(-1, 2 * HEAD_DIM), w_out_t)
    return project_and_reduce(context, wo.reshape(-1, cols))


def solution(mesh):
    spec = P("blk", "fsdp")
    return jax.shard_map(
        shards, mesh=mesh, in_specs=(spec,) * 5,
        out_specs=P(("blk", "fsdp"), None), check_vma=False,
    )
```
